32 devices in a mesh: section: 2 (over core), dp: 16 (over z, y, x).
Axes of the slice: x: 2, y: 2, z: 4, core: 2. Of those that a mesh axis runs over, the one named last changes fastest.
Arguments:
- tokens: bfloat16 [32, 128, 1536], P('dp'), may hold values from -6 to 6
- cotangent: bfloat16 [32, 128, 1536], P('dp'), may hold values from -6 to 6
- segments: int32 [32, 128], P('dp'), may hold values from 0 to 2, never falling along the last dimension, each value on 1 to 64 neighbouring positions
- gain_attn: bfloat16 [2, 1536], P('section', 'dp'), may hold values from 0.099609375 to 1.8984375
- w_qkv: bfloat16 [2, 1536, 3072], P('section', 'dp'), may hold values from -0.15625 to 0.15625
- w_out: bfloat16 [2, 1536, 1536], P('section', 'dp'), may hold values from -0.875 to 0.875
- gain_mlp: bfloat16 [2, 1536], P('section', 'dp'), may hold values from 0.099609375 to 1.8984375
- w_gate_up: bfloat16 [2, 1536, 8192], P('section', 'dp'), may hold values from -0.15625 to 0.15625
- w_down: bfloat16 [2, 4096, 1536], P('section', 'dp'), may hold values from -0.1875 to 0.1875
Outputs:
- activations: bfloat16 [2, 32, 128, 1536], P('section', 'dp')
- input_grads: float32 [2, 32, 128, 1536], P('section', 'dp')
- grad_gain_attn: float32 [2, 1536], P('section', 'dp')
- grad_w_qkv: float32 [2, 1536, 3072], P('section', 'dp')
- grad_w_out: float32 [2, 1536, 1536], P('section', 'dp')
- grad_gain_mlp: float32 [2, 1536], P('section', 'dp')
- grad_w_gate_up: float32 [2, 1536, 8192], P('section', 'dp')
- grad_w_down: float32 [2, 4096, 1536], P('section', 'dp')
The draws below stay inside these ranges and needn't reach their ends.
Inputs may be any that keep to these rules, and one draw needn't show every extreme that they name: `segments`: along each sequence the segment numbers never fall; one segment covers at most 64 positions of a sequence.
All inputs are finite; a program needn't handle non-finite values.
Results may differ from the reference program's by a relative error of at most 0.025.
Values may be sent and summed in bfloat16 or wider, within the bound.
No kernel may reach another device: no remote copies, remote signals or barrier semaphores. Data moves between devices by JAX's collectives and lax.ppermute only.
A program may use at most 576 MiB of HBM per device.

```python
import math
import jax
import jax.numpy as jnp
import numpy as np
from jax import lax

D = 1536
HEADS = 16
KV_HEADS = 8
HEAD_WIDTH = 96
FF = 4096
SEQ = 128
DOCS = 3
ATT = 1536
QKV = 3072
SEQS = 32
N_SECTION = 2


def block_scale(own_key, extent, shards, least, top_value):
    loudness = 1.0
    for position, shards_of in shards:
        steps = jax.random.uniform(jax.random.fold_in(jax.random.fold_in(own_key, 6), position), (shards_of,), jnp.float32, least / len(shards), top_value / len(shards))
        loudness = loudness * jnp.repeat(jnp.exp(steps), extent[position] // shards_of).reshape((-1,) + (1,) * (len(extent) - 1 - position))
    return loudness


def profile(amount, total, reach, lean):
    weights = [(1 << 20) // math.isqrt(standing ** lean) + 1 for standing in range(2, amount + 1)]
    surplus, given = total - reach - (amount - 1), [1] * (amount - 1)
    while surplus > 0:
        candidates = [i for i in range(amount - 1) if given[i] < reach]
        whole, left = sum([weights[i] for i in candidates]), surplus
        for i in candidates:
            more = min(reach - given[i], max(1, left * weights[i] // whole), surplus)
            given[i] = given[i] + more
            surplus = surplus - more
    return np.array([reach] + given)


def uneven(rng, amount, total, bound, slope):
    if amount == 2:
        one = jax.random.randint(rng, (), max(1, total - bound), min(bound, total - 1) + 1)
        return jnp.stack([one, total - one])
    lengths = jnp.asarray(profile(amount, total, bound, slope), jnp.int32)
    pairs = (amount - 1) // 2
    source_of, sink = lengths[1:1 + 2 * pairs:2], lengths[2:2 + 2 * pairs:2]
    slack = jnp.minimum(source_of - 1, bound - sink)
    passed = jax.random.randint(jax.random.fold_in(rng, 1), (pairs,), 0, 1 << 20) % (slack + 1)
    lengths = lengths.at[1:1 + 2 * pairs:2].set(source_of - passed).at[2:2 + 2 * pairs:2].set(sink + passed)
    return lengths[jax.random.permutation(jax.random.fold_in(rng, 2), amount)]


def bell_draw(stream_key, shape, spread, most, shards=(), kind=jnp.bfloat16):
    entries = jax.random.normal(stream_key, shape, jnp.float32) * spread
    if len(shards) > 0:
        entries = block_scale(stream_key, shape, shards, -0.22, 0.18) * entries
    return jnp.clip(entries, min=-most, max=most).astype(kind)


def setup_inputs(seed: int = 0) -> dict:
    streams_of = jax.random.split(jax.random.key(seed), 10)
    tokens = bell_draw(streams_of[0], (SEQS, SEQ, D), 1.0, 6.0, ((0, 16),))
    cotangent = bell_draw(streams_of[1], (SEQS, SEQ, D), 1.0, 6.0, ((0, 16),))
    segments = jax.vmap(lambda own: jnp.searchsorted(jnp.cumsum(uneven(own, DOCS, SEQ, SEQ // 2, 0)), jnp.arange(SEQ), side="right"))(jax.random.split(streams_of[2], SEQS)).reshape((SEQS, SEQ)).astype(jnp.int32)
    gain_attn = jnp.clip(1.0 + 0.18 * jax.random.normal(streams_of[3], (N_SECTION, D), jnp.float32), 0.099609375, 1.8984375).astype(jnp.bfloat16)
    w_qkv = bell_draw(streams_of[4], (N_SECTION, D, QKV), D ** -0.5, 0.15625, ((0, 2), (1, 16)))
    w_out = bell_draw(streams_of[5], (N_SECTION, ATT, D), (D // 32) ** -0.5, 0.875, ((0, 2), (1, 16)))
    gain_mlp = jnp.clip(1.0 + 0.18 * jax.random.normal(streams_of[6], (N_SECTION, D), jnp.float32), 0.099609375, 1.8984375).astype(jnp.bfloat16)
    w_gate_up = bell_draw(streams_of[7], (N_SECTION, D, 2 * FF), D ** -0.5, 0.15625, ((0, 2), (1, 16)))
    w_down = bell_draw(streams_of[8], (N_SECTION, FF, D), (FF // 4) ** -0.5, 0.1875, ((0, 2), (1, 16)))
    return {"tokens": tokens, "cotangent": cotangent, "segments": segments, "gain_attn": gain_attn, "w_qkv": w_qkv, "w_out": w_out, "gain_mlp": gain_mlp, "w_gate_up": w_gate_up, "w_down": w_down}


rms_eps = 1e-05
rope_base = 10000.0

@jax.custom_vjp
def low(v):
    return lax.optimization_barrier(v.astype(jnp.bfloat16)).astype(jnp.float32)

@jax.custom_vjp
def low_back(v):
    return v

def low_keep(v):
    return (low(v), None)

def low_pass(kept, grad):
    return (grad,)

def back_keep(v):
    return (v, None)

def back_low(kept, grad):
    return (low(grad),)
low.defvjp(low_keep, low_pass)
low_back.defvjp(back_keep, back_low)

def exact_dot(left, right):
    return jnp.dot(left, right, precision=lax.Precision.HIGHEST)

def rms_scale(value):
    return lax.rsqrt(lax.optimization_barrier(jnp.mean(value * value, axis=-1, keepdims=True)) + rms_eps)

def rotary(labels):
    length = labels.shape[0]
    same_doc = labels[:, None] == labels[None, :]
    indices = jnp.arange(length)
    before = indices[None, :] < indices[:, None]
    places = lax.optimization_barrier(jnp.sum(jnp.where(same_doc & before, 1, 0), axis=1)).astype(jnp.float32)
    half_dim = HEAD_WIDTH // 2
    frequency = rope_base ** (-jnp.arange(half_dim, dtype=jnp.float32) / half_dim)
    angles = places[:, None] * frequency[None, :]
    allowed = same_doc & (indices[None, :] <= indices[:, None])
    return (jnp.cos(angles), jnp.sin(angles), allowed)

def rotate(heads, cos_table, sin_table):
    half_dim = heads.shape[-1] // 2
    front_half = heads[..., :half_dim]
    back_half = heads[..., half_dim:]
    cosine = cos_table[:, None, :]
    sine_rows = sin_table[:, None, :]
    return jnp.concatenate([front_half * cosine - back_half * sine_rows, back_half * cosine + front_half * sine_rows], axis=-1)

def block_layer(hidden, labels, params):
    gain_one, w_qkv, w_out, gain_two, w_gate_up, w_down = params
    length = hidden.shape[0]
    cos_table, sin_table, allowed = rotary(labels)
    normed = low(hidden * rms_scale(hidden) * gain_one)
    joined = low_back(exact_dot(normed, w_qkv))
    split_q = HEADS * HEAD_WIDTH
    split_k = split_q + KV_HEADS * HEAD_WIDTH
    query_rows = low(rotate(joined[:, :split_q].reshape(length, HEADS, HEAD_WIDTH), cos_table, sin_table))
    key_head_rows = low(rotate(joined[:, split_q:split_k].reshape(length, KV_HEADS, HEAD_WIDTH), cos_table, sin_table))
    value_rows = low(joined[:, split_k:].reshape(length, KV_HEADS, HEAD_WIDTH))
    grouped_queries = query_rows.reshape(length, KV_HEADS, HEADS // KV_HEADS, HEAD_WIDTH)
    logit_scores = low_back(jnp.einsum('yamf,naf->amyn', grouped_queries, key_head_rows, precision=lax.Precision.HIGHEST) * HEAD_WIDTH ** (-0.5))
    logit_scores = jnp.where(allowed[None, None], logit_scores, -1e+30)
    attention_weights = low(jax.nn.softmax(logit_scores, axis=-1))
    merged_heads = jnp.einsum('pjqc,cpu->qpju', attention_weights, value_rows, precision=lax.Precision.HIGHEST)
    merged_heads = low_back(low(merged_heads.reshape(length, HEADS * HEAD_WIDTH)))
    middle = hidden + low_back(exact_dot(merged_heads, w_out))
    second = low(middle * rms_scale(middle) * gain_two)
    gate_up = low_back(exact_dot(second, w_gate_up))
    inner_act = low(jax.nn.silu(gate_up[:, :FF]) * gate_up[:, FF:])
    return middle + low_back(exact_dot(inner_act, w_down))

def reference(tokens, cotangent, segments, gain_attn, w_qkv, w_out, gain_mlp, w_gate_up, w_down):
    inputs = tokens.astype(jnp.float32)
    params = tuple((item.astype(jnp.float32) for item in (gain_attn, w_qkv, w_out, gain_mlp, w_gate_up, w_down)))

    def section_pass(section_in, section_params):
        one_layer = jax.checkpoint(lambda hidden, labels: block_layer(hidden, labels, section_params))
        return lax.map(lambda pair_item: one_layer(pair_item[0], pair_item[1]), (section_in, segments))

    def whole_block(block_in, nudge_term, all_params):
        first_out = section_pass(block_in, tuple((item[0] for item in all_params)))
        handed = low_back(low(first_out)) + nudge_term
        last_out = section_pass(handed, tuple((item[1] for item in all_params)))
        return (last_out, first_out)
    nudge_zero = jnp.zeros(inputs.shape, jnp.float32)
    outputs, pullback, first_out = jax.vjp(whole_block, inputs, nudge_zero, params, has_aux=True)
    grad_input, grad_nudge, grad_params = pullback(cotangent.astype(jnp.float32))
    activations = jnp.stack([first_out, outputs]).astype(jnp.bfloat16)
    input_grads = jnp.stack([grad_input, grad_nudge])
    return (activations, input_grads, grad_params[0], grad_params[1], grad_params[2], grad_params[3], grad_params[4], grad_params[5])
```

```python
import jax
import jax.numpy as jnp
from jax import lax
from jax.sharding import Mesh, PartitionSpec as P

D = 1536
HEADS = 16
KV_HEADS = 8
HEAD_WIDTH = 96
FF = 4096

rms_eps = 1e-05
rope_base = 10000.0

AXES = ("section", "h", "g", "y", "x", "w")
DP = ("h", "g", "y", "x", "w")
bf16 = jnp.bfloat16
f32 = jnp.float32


def swap(value, axis):
    return lax.ppermute(value, axis, [(0, 1), (1, 0)])


def dot(a, b):
    return lax.dot_general(a, b, (((1,), (0,)), ((), ())), preferred_element_type=f32)


def dot_tn(a, b):
    return lax.dot_general(a, b, (((0,), (0,)), ((), ())), preferred_element_type=f32)


def dot_nt(a, b):
    return lax.dot_general(a, b, (((1,), (1,)), ((), ())), preferred_element_type=f32)


def to_order(value, rest):
    lead = value.shape[:-1]
    n = len(lead)
    split = value.reshape(lead + (2, 2, 2, 2, rest, -1))
    order = tuple(range(n)) + (n + 3, n + 4, n + 2, n, n + 1, n + 5)
    return split.transpose(order).reshape(value.shape)


def from_order(value, rest):
    lead = value.shape[:-1]
    n = len(lead)
    split = value.reshape(lead + (2, rest, 2, 2, 2, -1))
    order = tuple(range(n)) + (n + 3, n + 4, n + 2, n, n + 1, n + 5)
    return split.transpose(order).reshape(value.shape)


def by_bit(bit, mine, theirs, axis):
    first = jnp.where(bit == 0, mine, theirs)
    last = jnp.where(bit == 0, theirs, mine)
    return jnp.stack([first, last], axis=axis)


def pick(bit, value, axis):
    return lax.dynamic_index_in_dim(value, bit, axis, keepdims=False)


def relative(bit, value):
    half = value.shape[-1] // 2
    turned = jnp.concatenate([value[..., half:], value[..., :half]], axis=-1)
    return jnp.where(bit == 0, value, turned)


def gather2(value):
    return jnp.concatenate([value, swap(value, "g")], axis=0)


def scatter2(part):
    rows = part.shape[0] // 2
    return part[:rows] + swap(part[rows:].astype(bf16), "g").astype(f32)


def gather4(value):
    half = value.shape[0] // 2
    across_y = swap(value, "y")
    across_g = swap(value, "g")
    corner_a = swap(across_y[:half], "g")
    corner_b = swap(across_g[half:], "y")
    return jnp.concatenate([value, across_y, across_g, corner_a, corner_b], axis=0)


def scatter4(part):
    rows = part.shape[0] // 4
    half = rows // 2
    own, for_y, for_g, corner = (part[i * rows : (i + 1) * rows] for i in range(4))
    low = corner.astype(bf16)
    from_g = swap(low[:half], "g").astype(f32)
    from_y = swap(low[half:], "y").astype(f32)
    send_y = jnp.concatenate([for_y[:half] + from_g, for_y[half:]], axis=0).astype(bf16)
    send_g = jnp.concatenate([for_g[:half], for_g[half:] + from_y], axis=0).astype(bf16)
    return own + (swap(send_y, "y").astype(f32) + swap(send_g, "g").astype(f32))


def rms_scale(value):
    return lax.rsqrt(jnp.mean(value * value, axis=-1, keepdims=True) + rms_eps)


def norm_back(value, scale_rows, gain_row, incoming):
    unit_rows = value * scale_rows
    grad_gain = jnp.sum(incoming * unit_rows, axis=0)
    grad_unit = incoming * gain_row
    grad_value = scale_rows * (
        grad_unit - unit_rows * jnp.mean(grad_unit * unit_rows, axis=-1, keepdims=True)
    )
    return grad_value, grad_gain


def rotary(labels):
    length = labels.shape[-1]
    same_doc = labels[:, :, None] == labels[:, None, :]
    indices = jnp.arange(length)
    before = indices[None, :] < indices[:, None]
    places = jnp.sum(jnp.where(same_doc & before[None], 1, 0), axis=2).astype(f32)
    half_dim = HEAD_WIDTH // 2
    frequency = rope_base ** (-jnp.arange(half_dim, dtype=f32) / half_dim)
    angles = places[:, :, None] * frequency
    allowed = same_doc & (indices[None, :] <= indices[:, None])[None]
    return jnp.cos(angles), jnp.sin(angles), allowed


def rotate(heads, cos_table, sin_table):
    half_dim = HEAD_WIDTH // 2
    front = heads[..., :half_dim]
    back = heads[..., half_dim:]
    cosine = cos_table[:, :, None, :]
    sine = sin_table[:, :, None, :]
    return jnp.concatenate([front * cosine - back * sine, back * cosine + front * sine], axis=-1)


def split_heads(joined, seqs, length):
    q = joined[:, :384].reshape(seqs, length, 4, HEAD_WIDTH)
    k = joined[:, 384:576].reshape(seqs, length, 2, HEAD_WIDTH)
    v = joined[:, 576:].reshape(seqs, length, 2, HEAD_WIDTH)
    return q, k, v


def attention(joined, tables, seqs, length):
    cos_table, sin_table, allowed = tables
    q, k, v = split_heads(joined, seqs, length)
    q = rotate(q, cos_table, sin_table).astype(bf16).reshape(seqs, length, 2, 2, HEAD_WIDTH)
    k = rotate(k, cos_table, sin_table).astype(bf16)
    v = v.astype(bf16)
    scores = jnp.einsum("btxyd,buyd->bxytu", q, k, preferred_element_type=f32) * HEAD_WIDTH ** (-0.5)
    scores = jnp.where(allowed[:, None, None], scores, -1e30)
    peak = jnp.max(scores, axis=-1, keepdims=True)
    lse = peak + jnp.log(jnp.sum(jnp.exp(scores - peak), axis=-1, keepdims=True))
    probs = jnp.exp(scores - lse)
    mixed = jnp.einsum("bxytu,buyd->btxyd", probs.astype(bf16), v, preferred_element_type=f32)
    mixed = mixed.astype(bf16).reshape(seqs * length, 4 * HEAD_WIDTH)
    return mixed, (q, k, v, probs)


def attention_back(go, kept, tables, seqs, length):
    cos_table, sin_table, _ = tables
    q, k, v, probs = kept
    go = go.astype(bf16).reshape(seqs, length, 2, 2, HEAD_WIDTH)
    grad_v = jnp.einsum("bxytu,btxyd->buyd", probs.astype(bf16), go, preferred_element_type=f32)
    dp = jnp.einsum("btxyd,buyd->bxytu", go, v, preferred_element_type=f32)
    row = jnp.sum(dp * probs, axis=-1, keepdims=True)
    dsc = (probs * (dp - row)).astype(bf16)
    scale = HEAD_WIDTH ** (-0.5)
    grad_q = jnp.einsum("bxytu,buyd->btxyd", dsc, k, preferred_element_type=f32) * scale
    grad_k = jnp.einsum("bxytu,btxyd->buyd", dsc, q, preferred_element_type=f32) * scale
    rows = seqs * length
    grad_q = rotate(grad_q.reshape(seqs, length, 4, HEAD_WIDTH), cos_table, -sin_table)
    grad_k = rotate(grad_k, cos_table, -sin_table)
    return jnp.concatenate(
        [grad_q.reshape(rows, 384), grad_k.reshape(rows, 192), grad_v.reshape(rows, 192)], axis=1
    ).astype(bf16)


def shards(tokens, cotangent, segments, gain_attn, w_qkv, w_out, gain_mlp, w_gate_up, w_down):
    core = lax.axis_index("section")
    hb = lax.axis_index("h")
    xb = lax.axis_index("x")
    rest = lax.axis_size("w")
    length = tokens.shape[1]
    rows = w_qkv.shape[1]
    units = w_down.shape[1] // 2
    place = lax.axis_index(DP)

    def all_reduce(value):
        for axis in ("section", "g", "y", "x", "h"):
            value = value + swap(value, axis)
        return lax.psum(value, "w") if rest > 1 else value

    def over_w(value):
        return lax.all_gather(value, "w", axis=0) if rest > 1 else value[None]

    gains = jnp.zeros((2, 2, D), f32)
    own_gains = jnp.stack([gain_attn[0], gain_mlp[0]]).astype(f32)
    gains = lax.dynamic_update_slice(gains, own_gains[None], (core, 0, place * rows))
    gains = to_order(all_reduce(gains), rest)

    def quarter(part, order):
        return part.transpose(order)

    q = w_qkv[0, :, :D].reshape(rows, 2, 2, 2, 2, HEAD_WIDTH).transpose(1, 2, 0, 4, 3, 5)
    k = w_qkv[0, :, D : D + D // 2].reshape(rows, 2, 2, 192).transpose(1, 2, 0, 3)
    v = w_qkv[0, :, D + D // 2 :].reshape(rows, 2, 2, 192).transpose(1, 2, 0, 3)
    qkv = jnp.concatenate([q.reshape(4, rows, 384), k.reshape(4, rows, 192), v.reshape(4, rows, 192)], axis=2)
    qkv = lax.all_to_all(qkv, ("section", "g"), 0, 0, tiled=True).reshape(2, 2, rows, 768)

    out = lax.all_gather(to_order(w_out[0], rest), "section", axis=0)
    out = jnp.where(hb == core, out, swap(out, "h"))

    up = w_gate_up[0].reshape(rows, 2, 2, 2, 2, 2, rest, 2, units)
    up = up.transpose(7, 4, 3, 0, 1, 5, 6, 2, 8)
    slice_width = 2 * 2 * rest * 2 * units
    up = up.reshape(8, rows, slice_width)
    up = lax.all_to_all(up, ("section", "y", "g"), 0, 0, tiled=True).reshape(2, 2, 2, rows, slice_width)

    down = to_order(w_down[0], rest).reshape(2, units, D)
    down = lax.all_to_all(down, "section", 0, 0, tiled=True)

    def attn_weights(layer):
        part = by_bit(hb, qkv[layer], swap(qkv[layer], "h"), 0).reshape(4 * rows, 768)
        wide = lax.all_gather(part, ("x", "w", "y"), axis=0, tiled=True)
        tall = lax.all_gather(out[layer], ("x", "y", "w"), axis=0, tiled=True)
        return (wide, swap(wide, "section")), (tall, swap(tall, "section"))

    def mlp_weights(layer):
        part = by_bit(hb, up[layer], swap(up[layer], "h"), 1)
        part = over_w(part).reshape(D // 2, slice_width)
        other = swap(part, "x")
        tall = over_w(by_bit(hb, down[layer], swap(down[layer], "h"), 0)).reshape(rest * 2 * units, D)
        tall_other = swap(tall, "x")
        wide = ((part, other), (swap(part, "section"), swap(other, "section")))
        high = ((tall, tall_other), (swap(tall, "section"), swap(tall_other, "section")))
        return wide, high

    own = lax.dynamic_index_in_dim(segments, core, 0, keepdims=True)
    labels = gather2(own)
    tables = rotary(labels)

    def forward(hidden, attn, mlp, gain):
        (wide_m, wide_t), (tall_m, tall_t) = attn
        scale_one = rms_scale(hidden)
        normed = gather2((hidden * scale_one * gain[0]).astype(bf16))
        mixed_m, kept_m = attention(dot(normed, wide_m), tables, 2, length)
        mixed_t, kept_t = attention(dot(normed, wide_t), tables, 2, length)
        middle = hidden + scatter2(dot(mixed_m, tall_m) + dot(mixed_t, tall_t))
        scale_two = rms_scale(middle)
        second = (middle * scale_two * gain[1]).astype(bf16)
        second = gather4(relative(xb, second))
        halves = (second[:, : D // 2], second[:, D // 2 :])
        parts = []
        total = 0.0
        for (near, far), (tall, tall_other) in zip(*mlp):
            gate_up = dot(halves[0], near) + dot(halves[1], far)
            gate = gate_up[:, : slice_width // 2]
            lift = gate_up[:, slice_width // 2 :]
            inner = relative(xb, (jax.nn.silu(gate) * lift).astype(bf16))
            mid = inner.shape[1] // 2
            total = total + dot(inner[:, :mid], tall) + dot(inner[:, mid:], tall_other)
            parts.append((gate, lift, inner))
        result = middle + scatter4(total)
        kept = (hidden, scale_one, normed, (mixed_m, mixed_t), (kept_m, kept_t), middle, scale_two, halves, parts)
        return result, kept

    def combine(mine, theirs):
        return (mine + swap(theirs.astype(bf16), "section").astype(f32)).astype(bf16)

    def over_h(value, axis):
        mine = pick(hb, value, axis)
        return mine.astype(f32) + swap(pick(1 - hb, value, axis), "h").astype(f32)

    def scatter_w(value):
        if rest == 1:
            return value
        return lax.psum_scatter(value, "w", scatter_dimension=0, tiled=True)

    def backward(grad, kept, attn, mlp, gain):
        (wide_m, wide_t), (tall_m, tall_t) = attn
        hidden, scale_one, normed, mixed, kept_attn, middle, scale_two, halves, parts = kept
        low = gather4(grad.astype(bf16))
        grad_near = 0.0
        grad_far = 0.0
        pieces = []
        for ((near, far), (tall, tall_other)), (gate, lift, inner) in zip(zip(*mlp), parts):
            mid = inner.shape[1] // 2
            down_near = dot_tn(inner[:, :mid], low)
            down_far = dot_tn(inner[:, mid:], low)
            gi = jnp.concatenate([dot_nt(low, tall), dot_nt(low, tall_other)], axis=1)
            gi = relative(xb, gi)
            sig = jax.nn.sigmoid(gate)
            g_gate = gi * lift * sig * (1.0 + gate * (1.0 - sig))
            g_up = gi * gate * sig
            gg = jnp.concatenate([g_gate, g_up], axis=1).astype(bf16)
            pieces.append((down_near, down_far, dot_tn(halves[0], gg), dot_tn(halves[1], gg)))
            grad_near = grad_near + dot_nt(gg, near)
            grad_far = grad_far + dot_nt(gg, far)
        gs = relative(xb, scatter4(jnp.concatenate([grad_near, grad_far], axis=1)))

        down_near, down_far, up_near, up_far = (combine(a, b) for a, b in zip(*pieces))
        grad_down = down_near.astype(f32) + swap(down_far, "x").astype(f32)
        grad_up = up_near.astype(f32) + swap(up_far, "x").astype(f32)
        grad_down = scatter_w(grad_down.astype(bf16)).reshape(2, units, D)
        grad_down = over_h(grad_down, 0).astype(bf16)
        grad_up = scatter_w(grad_up.astype(bf16)).reshape(2, 2, 2, rows, slice_width)
        grad_up = over_h(grad_up, 1).astype(bf16)

        gm, gain_two = norm_back(middle, scale_two, gain[1], gs)
        gm = gm + grad
        gmb = gather2(gm.astype(bf16))
        grad_out = combine(dot_tn(mixed[0], gmb), dot_tn(mixed[1], gmb))
        grad_out = lax.psum_scatter(grad_out, ("x", "y", "w"), scatter_dimension=0, tiled=True)
        grad_out = (grad_out.astype(f32) + swap(grad_out, "h").astype(f32)).astype(bf16)
        gq_m = attention_back(dot_nt(gmb, tall_m), kept_attn[0], tables, 2, length)
        gq_t = attention_back(dot_nt(gmb, tall_t), kept_attn[1], tables, 2, length)
        gn = scatter2(dot_nt(gq_m, wide_m) + dot_nt(gq_t, wide_t))
        grad_qkv = combine(dot_tn(normed, gq_m), dot_tn(normed, gq_t))
        grad_qkv = lax.psum_scatter(grad_qkv, ("x", "w", "y"), scatter_dimension=0, tiled=True)
        grad_qkv = over_h(grad_qkv.reshape(2, 2, rows, 768), 0).astype(bf16)
        grad_in, gain_one = norm_back(hidden, scale_one, gain[0], gn)
        return grad_in + gm, (grad_qkv, grad_out, grad_up, grad_down, jnp.stack([gain_one, gain_two]))

    start = to_order(pick(core, tokens, 0).astype(f32), rest)
    attn = [attn_weights(0), None]
    mlp = [mlp_weights(0), None]
    attn[1] = attn_weights(1)
    mlp[1] = mlp_weights(1)
    first, kept_first = forward(start, attn[0], mlp[0], gains[0])
    handed = first.astype(bf16)
    last, kept_last = forward(handed.astype(f32), attn[1], mlp[1], gains[1])
    acts = from_order(jnp.stack([handed, last.astype(bf16)]), rest)
    acts = lax.all_to_all(acts, "section", 0, 0, tiled=True)[None]

    grad = to_order(pick(core, cotangent, 0).astype(f32), rest)
    grad_last, grads_last = backward(grad, kept_last, attn[1], mlp[1], gains[1])
    handed_back = grad_last.astype(bf16).astype(f32)
    grad_first, grads_first = backward(handed_back, kept_first, attn[0], mlp[0], gains[0])
    input_grads = from_order(jnp.stack([grad_first, grad_last]), rest)
    input_grads = lax.all_to_all(input_grads, "section", 0, 0, tiled=True)[None]

    both = [jnp.stack(pair) for pair in zip(grads_first, grads_last)]
    grad_qkv = lax.all_to_all(both[0].reshape(4, rows, 768), ("section", "g"), 0, 0, tiled=True)
    gq = grad_qkv[:, :, :384].reshape(2, 2, rows, 2, 2, HEAD_WIDTH).transpose(2, 0, 1, 4, 3, 5)
    gk = grad_qkv[:, :, 384:576].transpose(1, 0, 2)
    gv = grad_qkv[:, :, 576:].transpose(1, 0, 2)
    grad_qkv = jnp.concatenate([part.reshape(rows, -1) for part in (gq, gk, gv)], axis=1).astype(f32)[None]

    mine = pick(core, both[1], 0)
    grad_out = jnp.where(hb == core, mine, swap(pick(1 - core, both[1], 0), "section"))
    grad_out = from_order(grad_out.astype(f32), rest)[None]

    grad_up = lax.all_to_all(both[2].reshape(8, rows, slice_width), ("section", "y", "g"), 0, 0, tiled=True)
    grad_up = grad_up.reshape(2, 2, 2, rows, 2, 2, rest, 2, units).transpose(3, 4, 7, 2, 1, 5, 6, 0, 8)
    grad_up = grad_up.reshape(rows, 2 * FF).astype(f32)[None]

    grad_down = lax.all_to_all(both[3], "section", 0, 0, tiled=True).reshape(2 * units, D)
    grad_down = from_order(grad_down.astype(f32), rest)[None]

    gain_sums = from_order(all_reduce(both[4]), rest)
    gain_sums = lax.dynamic_slice(gain_sums, (core, 0, place * rows), (1, 2, rows))
    return (
        acts,
        input_grads,
        gain_sums[:, 0],
        grad_qkv,
        grad_out,
        gain_sums[:, 1],
        grad_up,
        grad_down,
    )


def solution(mesh):
    count = mesh.shape["dp"]
    wide = Mesh(mesh.devices.reshape(2, 2, 2, 2, 2, count // 16), AXES)
    in_specs = (
        P(DP, None, None),
        P(DP, None, None),
        P(DP, None),
        P("section", DP),
        P("section", DP, None),
        P("section", DP, None),
        P("section", DP),
        P("section", DP, None),
        P("section", DP, None),
    )
    out_specs = (
        P("section", DP, None, None),
        P("section", DP, None, None),
        P("section", DP),
        P("section", DP, None),
        P("section", DP, None),
        P("section", DP),
        P("section", DP, None),
        P("section", DP, None),
    )
    return jax.shard_map(shards, mesh=wide, in_specs=in_specs, out_specs=out_specs, check_vma=False)
```
